1024 devices in a mesh: dp: 4 (over y_hi), blk: 32 (over y_lo, z), head: 8 (over x, core).
Axes of the slice: x: 4, y: 8 (y_hi: 4, y_lo: 2; y = y_hi * 2 + y_lo), z: 16, core: 2. Of those that a mesh axis runs over, the one named last changes fastest.
Arguments:
- queries: bfloat16 [65536, 2048], P(('dp', 'blk', 'head')), parts along dimension 0, may hold values from -5 to 5
- key_states: bfloat16 [65536, 2048], P(('dp', 'blk', 'head')), parts along dimension 0, may hold values from -5 to 5
- value_states: bfloat16 [65536, 2048], P(('dp', 'blk', 'head')), parts along dimension 0, may hold values from -6 to 6
- upstream: bfloat16 [65536, 2048], P(('dp', 'blk'), 'head'), parts along dimension 0, may hold values from -6 to 6
- clip_lengths: int32 [128], P('dp'), parts along dimension 0, may hold values from 1 to 1024, 16384 in all
Outputs:
- attended: bfloat16 [65536, 2048], P(('dp', 'blk'), 'head'), parts along dimension 0
- query_grads: bfloat16 [65536, 2048], P(('dp', 'blk'), 'head'), parts along dimension 0
- key_grads: bfloat16 [65536, 2048], P(('dp', 'blk'), 'head'), parts along dimension 0
- value_grads: bfloat16 [65536, 2048], P(('dp', 'blk'), 'head'), parts along dimension 0
The draws below stay inside these ranges and needn't reach their ends.
There are 4 independent parts, one for each index of `dp`. The reference program is written for one: setup_inputs(seed, part) draws one part's arguments, and reference() takes and returns one part's arrays. A program takes and returns all parts, laid end to end along the dimension named above; each array names one. Nothing has to cross between parts.
Inputs may be any that keep to these rules, and one draw needn't show every extreme that they name: `clip_lengths`: 32 clip lengths that sum to 16384; the longest has exactly 1024 tokens.
All inputs are finite; a program needn't handle non-finite values.
Results may differ from the reference program's by a relative error of at most 0.015.
Values may be sent and summed in bfloat16 or wider, within the bound.
A program may use at most 32 MiB of HBM per device.

```python
import math
import jax
import jax.numpy as jnp
import numpy as np
from jax import lax

HEADS = 16
HEAD_DIM = 128
BLOCK = 512
SEQ = 16384
MOST = 1024
CLIPS = 32


def draw_queries(key, part):
    noise_key = jax.random.fold_in(jax.random.fold_in(key, 1), 0)
    drawn = jnp.clip(jax.random.normal(noise_key, (SEQ, HEADS * HEAD_DIM), jnp.float32), -5.0, 5.0)
    return drawn.astype(jnp.bfloat16)


def draw_key_states(key, part):
    noise_key = jax.random.fold_in(jax.random.fold_in(key, 2), 0)
    drawn = jnp.clip(jax.random.normal(noise_key, (SEQ, HEADS * HEAD_DIM), jnp.float32), -5.0, 5.0)
    return drawn.astype(jnp.bfloat16)


def steps_of(key, shape, shards, smallest, largest):
    factor_of, own = 1.0, jax.random.fold_in(key, 6)
    for dim, parts in shards:
        steps = jnp.exp(jax.random.uniform(jax.random.fold_in(own, dim), (parts,), jnp.float32, smallest / len(shards), largest / len(shards)))
        factor_of = factor_of * jnp.repeat(steps, shape[dim] // parts).reshape([-1 if axis == dim else 1 for axis in range(len(shape))])
    return factor_of


def length_profile(amount, total, limit, skew):
    portions = [(1 << 20) // math.isqrt(rank ** skew) + 1 for rank in range(2, amount + 1)]
    spare, given = total - limit - (amount - 1), [1] * (amount - 1)
    while spare > 0:
        movable = [i for i in range(amount - 1) if given[i] < limit]
        whole, remaining = sum([portions[i] for i in movable]), spare
        for i in movable:
            extra = min(limit - given[i], max(1, remaining * portions[i] // whole), spare)
            given[i] = given[i] + extra
            spare = spare - extra
    return np.array([limit] + given)


def uneven_parts(own_key, amount, total, bound, skew):
    if amount == 2:
        one = jax.random.randint(own_key, (), max(1, total - bound), min(bound, total - 1) + 1)
        return jnp.stack([one, total - one])
    lengths = jnp.asarray(length_profile(amount, total, bound, skew), jnp.int32)
    couples = (amount - 1) // 2
    source_of, taker = lengths[1:1 + 2 * couples:2], lengths[2:2 + 2 * couples:2]
    margin = jnp.minimum(source_of - 1, bound - taker)
    passed = jax.random.randint(jax.random.fold_in(own_key, 1), (couples,), 0, 1 << 20) % (margin + 1)
    lengths = lengths.at[1:1 + 2 * couples:2].set(source_of - passed).at[2:2 + 2 * couples:2].set(taker + passed)
    return lengths[jax.random.permutation(jax.random.fold_in(own_key, 2), amount)]


def noise(stream_key, shape, spread, reach, shards=(), held_as=jnp.bfloat16):
    result = spread * jax.random.normal(stream_key, shape, jnp.float32)
    if shards:
        result = result * steps_of(stream_key, shape, shards, -0.22, 0.18)
    return jnp.clip(result, -reach, reach).astype(held_as)


def setup_inputs(seed: int = 0, part: int = 0) -> dict:
    seeds = jax.random.split(jax.random.key(seed), 6)
    part_keys = jax.random.split(jax.random.fold_in(seeds[5], part), 6)
    return {
        "queries": draw_queries(jax.random.fold_in(jax.random.fold_in(seeds[5], part), 71), part),
        "key_states": draw_key_states(jax.random.fold_in(jax.random.fold_in(seeds[5], part), 71), part),
        "value_states": noise(part_keys[2], (SEQ, HEADS * HEAD_DIM), 1.0, 6.0, ((0, 256),)),
        "upstream": noise(part_keys[3], (SEQ, HEADS * HEAD_DIM), 1.0, 6.0, ((0, 32), (1, 8))),
        "clip_lengths": uneven_parts(part_keys[4], CLIPS, SEQ, MOST, 1).astype(jnp.int32),
    }


masked_fill = -1.0e30


def clip_index(clip_ends, positions, seq_total):
    counted = jnp.sum((positions[:, None] >= clip_ends[None, :]).astype(jnp.int32), axis=1)
    inside = (positions >= 0) & (positions < seq_total)
    return jnp.where(inside, counted, -1).astype(jnp.int32)


def rounded(values_in):
    return lax.optimization_barrier(values_in.astype(jnp.bfloat16)).astype(jnp.float32)


def window_pass(query_tile, key_tile, value_tile, upstream_tile, query_ids, key_ids):
    score_scale = HEAD_DIM ** -0.5
    query_wide = query_tile.astype(jnp.float32)
    key_wide = key_tile.astype(jnp.float32)
    value_wide = value_tile.astype(jnp.float32)
    upstream_wide = upstream_tile.astype(jnp.float32)
    same_clip = (query_ids[:, None] == key_ids[None, :])[None]
    scores = score_scale * jnp.einsum("qhe,khe->hqk", query_wide, key_wide)
    scores = jnp.where(same_clip, scores, masked_fill)
    row_max = jnp.max(scores, axis=2, keepdims=True)
    totals = jnp.sum(jnp.where(same_clip, jnp.exp(scores - row_max), 0.0), axis=2, keepdims=True)
    log_norm = row_max + jnp.log(totals)
    chances = jnp.where(same_clip, jnp.exp(scores - log_norm), 0.0)
    weights = rounded(chances)
    attended = rounded(jnp.einsum("hqk,khe->qhe", weights, value_wide))
    offsets = jnp.sum(upstream_wide * attended, axis=2)
    dchances = jnp.einsum("qhe,khe->hqk", upstream_wide, value_wide)
    dscores = rounded(chances * (dchances - jnp.transpose(offsets)[:, :, None]))
    query_part = score_scale * jnp.einsum("hqk,khe->qhe", dscores, key_wide)
    key_part = score_scale * jnp.einsum("hqk,qhe->khe", dscores, query_wide)
    value_part = jnp.einsum("hqk,qhe->khe", weights, upstream_wide)
    return attended, query_part, key_part, value_part


def reference(queries, key_states, value_states, upstream, clip_lengths):
    feature_width = HEADS * HEAD_DIM
    block_count = SEQ // BLOCK
    clip_ends = jnp.cumsum(clip_lengths).astype(jnp.int32)
    padded_keys = jnp.pad(key_states, ((BLOCK, 0), (0, 0)))
    padded_values = jnp.pad(value_states, ((BLOCK, 0), (0, 0)))
    positions = jnp.arange(SEQ + BLOCK, dtype=jnp.int32) - BLOCK
    padded_ids = clip_index(clip_ends, positions, SEQ)

    def advance(totals, block_index):
        row_start = (block_index * BLOCK).astype(jnp.int32)
        query_tile = lax.dynamic_slice_in_dim(queries, row_start, BLOCK, 0).reshape(BLOCK, HEADS, HEAD_DIM)
        upstream_tile = lax.dynamic_slice_in_dim(upstream, row_start, BLOCK, 0).reshape(BLOCK, HEADS, HEAD_DIM)
        key_tile = lax.dynamic_slice_in_dim(padded_keys, row_start, 2 * BLOCK, 0).reshape(2 * BLOCK, HEADS, HEAD_DIM)
        value_tile = lax.dynamic_slice_in_dim(padded_values, row_start, 2 * BLOCK, 0).reshape(2 * BLOCK, HEADS, HEAD_DIM)
        query_ids = lax.dynamic_slice_in_dim(padded_ids, row_start + BLOCK, BLOCK, 0)
        key_ids = lax.dynamic_slice_in_dim(padded_ids, row_start, 2 * BLOCK, 0)
        attended, query_part, key_part, value_part = window_pass(query_tile, key_tile, value_tile, upstream_tile, query_ids, key_ids)
        update = jnp.stack([key_part, value_part]).reshape(2, 2 * BLOCK, feature_width)
        window = lax.dynamic_slice_in_dim(totals, row_start, 2 * BLOCK, 1)
        totals = lax.dynamic_update_slice_in_dim(totals, window + update, row_start, 1)
        return totals, (attended.reshape(BLOCK, feature_width), query_part.reshape(BLOCK, feature_width))

    start_totals = jnp.zeros((2, SEQ + BLOCK, feature_width), jnp.float32)
    totals, collected = lax.scan(advance, start_totals, jnp.arange(block_count, dtype=jnp.int32))
    attended = collected[0].reshape(SEQ, feature_width).astype(jnp.bfloat16)
    query_grads = collected[1].reshape(SEQ, feature_width).astype(jnp.bfloat16)
    grad_pairs = totals[:, BLOCK:]
    return attended, query_grads, grad_pairs[0].astype(jnp.bfloat16), grad_pairs[1].astype(jnp.bfloat16)
```

```python
import functools

import jax
import jax.numpy as jnp
from jax import lax
from jax.experimental import pallas as pl
from jax.experimental.pallas import tpu as pltpu
from jax.sharding import PartitionSpec as P

HEAD_DIM = 128
SCALE = HEAD_DIM ** (-0.5)
LOG2E = 1.4426950408889634
MESH = pl.DeviceIdType.MESH
MASKED = -1e30
K, V, Q, U = 0, 1, 2, 3
PARTNERS = ((0, 1), (1, 0), (3, 0), (1, 1), (3, 1), (2, 0), (2, 1))

NT = (((1,), (1,)), ((), ()))
TN = (((0,), (0,)), ((), ()))


def dot(a, b, dims=(((1,), (0,)), ((), ()))):
    return lax.dot_general(a, b, dims, preferred_element_type=jnp.float32)


def kernel(
    heads_here, blocks, chunk,
    q_hbm, k_hbm, v_hbm, u_hbm, lengths,
    att_ref, dq_ref, dk_ref, dv_ref,
    ks, vs, qs, us, kid, qid, stat_out, stat_in, dk_acc, dv_acc,
    own_sem, sx, rx, sz, rz, ss, rs,
):
    part, blk, me = lax.axis_index("dp"), lax.axis_index("blk"), lax.axis_index("head")
    group = lax.axis_size("head")
    rows = q_hbm.shape[0]
    block = rows * group
    wide = heads_here * HEAD_DIM
    chip, core = me // 2, lax.rem(me, 2)
    chips = group // 2
    after, before = lax.rem(blk + 1, blocks), lax.rem(blk + blocks - 1, blocks)

    def to(dx, dc):
        return lax.rem(chip + dx, chips) * 2 + lax.rem(core + dc, 2)

    def source(dx, dc):
        return lax.rem(chip + chips - dx, chips) * 2 + lax.rem(core + dc, 2)

    barrier = pltpu.get_barrier_semaphore()
    for dx, dc in PARTNERS:
        pl.semaphore_signal(barrier, inc=1, device_id=(part, blk, to(dx, dc)), device_id_type=MESH)
    for other in (after, before):
        pl.semaphore_signal(barrier, inc=1, device_id=(part, other, me), device_id_type=MESH)
    pl.semaphore_wait(barrier, len(PARTNERS) + 2)

    inputs = (k_hbm, v_hbm, q_hbm)
    held = (ks, vs, qs)

    def columns(owner, h):
        return pl.ds(pl.multiple_of(owner * wide + h * HEAD_DIM, HEAD_DIM), HEAD_DIM)

    def place(owner, second):
        return pl.ds(pl.multiple_of(owner * rows + second * block, rows), rows)

    def own_half(a):
        return 1 if a in (K, V) else 0

    def neighbour(a):
        return (part, after, me) if a in (K, V) else (part, before, me)

    def x_copy(a, h, dx, dc, owner, target):
        return pltpu.make_async_remote_copy(
            src_ref=inputs[a].at[:, columns(target, h)],
            dst_ref=held[a].at[h, place(owner, own_half(a)), :],
            send_sem=sx.at[a, h],
            recv_sem=rx.at[a, h, dx * 2 + dc],
            device_id=(part, blk, target),
            device_id_type=MESH,
        )

    def z_copy(a, h, owner, src):
        return pltpu.make_async_remote_copy(
            src_ref=src,
            dst_ref=held[a].at[h, place(owner, 1 - own_half(a)), :],
            send_sem=sz.at[a, h],
            recv_sem=rz.at[a, h],
            device_id=neighbour(a),
            device_id_type=MESH,
        )

    def z_all(a, h):
        ref = us if a == U else held[a]
        half = 0 if a in (K, V) else 1
        whole = ref.at[h, half * block : (half + 1) * block, :]
        return pltpu.make_async_remote_copy(
            src_ref=whole, dst_ref=whole, send_sem=sz.at[a, h], recv_sem=rz.at[a, h],
            device_id=neighbour(a), device_id_type=MESH,
        )

    def x_sent(a, h):
        part_of = held[a].at[h, 0 : len(PARTNERS) * rows, :]
        return pltpu.make_async_remote_copy(
            src_ref=part_of, dst_ref=part_of, send_sem=sx.at[a, h], recv_sem=rx.at[a, h, 0],
            device_id=(part, blk, to(0, 1)), device_id_type=MESH,
        )

    own = []
    for h in range(heads_here):
        for a in (K, V, Q):
            for dx, dc in PARTNERS:
                x_copy(a, h, dx, dc, me, to(dx, dc)).start()
            z_copy(a, h, me, inputs[a].at[:, columns(me, h)]).start()
        pltpu.make_async_remote_copy(
            src_ref=u_hbm.at[:, h * HEAD_DIM : (h + 1) * HEAD_DIM],
            dst_ref=us.at[h, block : 2 * block, :],
            send_sem=sz.at[U, h],
            recv_sem=rz.at[U, h],
            device_id=neighbour(U),
            device_id_type=MESH,
        ).start()
        for a in (K, V, Q):
            own.append(pltpu.make_async_copy(
                inputs[a].at[:, columns(me, h)],
                held[a].at[h, place(me, own_half(a)), :], own_sem.at[a, h]))
        own.append(pltpu.make_async_copy(
            u_hbm.at[:, h * HEAD_DIM : (h + 1) * HEAD_DIM], us.at[h, 0:block, :], own_sem.at[U, h]))
    for copy in own:
        copy.start()

    spread = 3 * block
    positions = (blk - 1) * block + lax.broadcasted_iota(jnp.int32, (1, spread), 1)
    counted = jnp.zeros((1, spread), jnp.int32)
    end = jnp.int32(0)
    for c in range(lengths.shape[0]):
        end = end + lengths[c]
        counted = counted + jnp.where(positions >= end, 1, 0)
    inside = (positions >= 0) & (positions < blocks * block)
    ids = jnp.where(inside, counted, -1)
    qid[...] = jnp.broadcast_to(ids[:, block:], qid.shape)
    for c in range(2 * block // HEAD_DIM):
        one = jnp.broadcast_to(ids[:, c * HEAD_DIM : (c + 1) * HEAD_DIM], (HEAD_DIM, HEAD_DIM))
        turned = one.T
        for n in range(chunk // HEAD_DIM):
            kid[c * HEAD_DIM : (c + 1) * HEAD_DIM, n * HEAD_DIM : (n + 1) * HEAD_DIM] = turned

    for h in range(heads_here):
        for a in (K, V, Q):
            for dx, dc in PARTNERS:
                owner = source(dx, dc)
                x_copy(a, h, dx, dc, owner, me).wait_recv()
                z_copy(a, h, owner, held[a].at[h, place(owner, own_half(a)), :]).start()
    for copy in own:
        copy.wait()

    def main(h):
        for a in (K, V):
            z_all(a, h).wait_recv()
        side = slice(h * HEAD_DIM, (h + 1) * HEAD_DIM)
        dk_acc[h] = jnp.zeros_like(dk_acc[h])
        dv_acc[h] = jnp.zeros_like(dv_acc[h])

        def step(c, carry):
            at = pl.ds(pl.multiple_of(c * chunk, chunk), chunk)
            query, up = qs[h, at, :], us[h, at, :]
            key, value = ks[h], vs[h]
            same = kid[...] == qid[0:1, at]
            scores = jnp.where(same, dot(key, query, NT), MASKED)
            top = jnp.max(scores, axis=0, keepdims=True)
            powers = jnp.exp2((scores - top) * (SCALE * LOG2E))
            total = jnp.sum(powers, axis=0, keepdims=True)
            chances = powers * (1.0 / total)
            weights = chances.astype(jnp.bfloat16)
            attended = dot(value, weights, TN).T.astype(jnp.bfloat16)
            att_ref[at, side] = attended
            products = up.astype(jnp.float32) * attended.astype(jnp.float32)
            offsets = jnp.sum(products.T, axis=0, keepdims=True)
            stat_out[h, 0:1, at] = top * (SCALE * LOG2E) + jnp.log2(total)
            stat_out[h, 1:2, at] = offsets
            dscores = (chances * (dot(value, up, NT) - offsets)).astype(jnp.bfloat16)
            dq_ref[at, side] = (dot(key, dscores, TN) * SCALE).T.astype(jnp.bfloat16)
            dv_acc[h] += dot(weights[block:], up)
            dk_acc[h] += dot(dscores[block:], query)
            return carry

        lax.fori_loop(0, block // chunk, step, 0)

    def stat_copy(h):
        return pltpu.make_async_remote_copy(
            src_ref=stat_out.at[h], dst_ref=stat_in.at[h], send_sem=ss.at[h], recv_sem=rs.at[h],
            device_id=(part, before, me), device_id_type=MESH,
        )

    def cross(h):
        z_all(Q, h).wait_recv()
        z_all(U, h).wait_recv()
        stat_copy(h).wait_recv()
        side = slice(h * HEAD_DIM, (h + 1) * HEAD_DIM)

        def step(c, carry):
            at = pl.ds(pl.multiple_of(c * chunk, chunk), chunk)
            there = pl.ds(pl.multiple_of(c * chunk + block, chunk), chunk)
            query, up = qs[h, there, :], us[h, there, :]
            key, value = ks[h, block:, :], vs[h, block:, :]
            same = kid[block:, :] == qid[0:1, there]
            powers = jnp.exp2(dot(key, query, NT) * (SCALE * LOG2E) - stat_in[h, 0:1, at])
            chances = jnp.where(same, powers, 0.0)
            dscores = chances * (dot(value, up, NT) - stat_in[h, 1:2, at])
            dv_acc[h] += dot(chances.astype(jnp.bfloat16), up)
            dk_acc[h] += dot(dscores.astype(jnp.bfloat16), query)
            return carry

        lax.fori_loop(0, block // chunk, step, 0)
        dk_ref[:, side] = (dk_acc[h] * SCALE).astype(jnp.bfloat16)
        dv_ref[:, side] = dv_acc[h].astype(jnp.bfloat16)

    for h in range(heads_here):
        main(h)
        stat_copy(h).start()
    for h in range(heads_here):
        cross(h)

    for h in range(heads_here):
        stat_copy(h).wait_send()
        for a in (K, V, Q):
            x_sent(a, h).wait_send()
        for a in (K, V, Q, U):
            z_all(a, h).wait_send()


def on_device(queries, key_states, value_states, upstream, clip_lengths):
    block, wide = upstream.shape
    heads_here = wide // HEAD_DIM
    chunk = 256
    group = lax.axis_size("head")
    blocks = lax.axis_size("blk")
    hbm = pl.BlockSpec(memory_space=pl.ANY)
    vmem = pl.BlockSpec(memory_space=pltpu.VMEM)
    out = jax.ShapeDtypeStruct((block, wide), jnp.bfloat16)
    return pl.pallas_call(
        functools.partial(kernel, heads_here, blocks, chunk),
        out_shape=(out,) * 4,
        in_specs=[hbm] * 4 + [pl.BlockSpec(memory_space=pltpu.SMEM)],
        out_specs=(vmem,) * 4,
        scratch_shapes=[
            pltpu.VMEM((heads_here, 2 * block, HEAD_DIM), jnp.bfloat16),
            pltpu.VMEM((heads_here, 2 * block, HEAD_DIM), jnp.bfloat16),
            pltpu.VMEM((heads_here, 2 * block, HEAD_DIM), jnp.bfloat16),
            pltpu.VMEM((heads_here, 2 * block, HEAD_DIM), jnp.bfloat16),
            pltpu.VMEM((2 * block, chunk), jnp.int32),
            pltpu.VMEM((8, 2 * block), jnp.int32),
            pltpu.VMEM((heads_here, 8, block), jnp.float32),
            pltpu.VMEM((heads_here, 8, block), jnp.float32),
            pltpu.VMEM((heads_here, block, HEAD_DIM), jnp.float32),
            pltpu.VMEM((heads_here, block, HEAD_DIM), jnp.float32),
            pltpu.SemaphoreType.DMA((4, heads_here)),
            pltpu.SemaphoreType.DMA((3, heads_here)),
            pltpu.SemaphoreType.DMA((3, heads_here, group)),
            pltpu.SemaphoreType.DMA((4, heads_here)),
            pltpu.SemaphoreType.DMA((4, heads_here)),
            pltpu.SemaphoreType.DMA((heads_here,)),
            pltpu.SemaphoreType.DMA((heads_here,)),
        ],
        compiler_params=pltpu.CompilerParams(collective_id=0, has_side_effects=True),
    )(queries, key_states, value_states, upstream, clip_lengths)


def solution(mesh):
    return jax.shard_map(
        on_device,
        mesh=mesh,
        in_specs=(
            P(("dp", "blk", "head"), None),
            P(("dp", "blk", "head"), None),
            P(("dp", "blk", "head"), None),
            P(("dp", "blk"), "head"),
            P("dp"),
        ),
        out_specs=(P(("dp", "blk"), "head"),) * 4,
        check_vma=False,
    )
```

```python
import functools

import jax
import jax.numpy as jnp
from jax import lax
from jax.experimental import pallas as pl
from jax.experimental.pallas import tpu as pltpu
from jax.sharding import PartitionSpec as P

HEAD_DIM = 128
SCALE = HEAD_DIM ** (-0.5)
LOG2E = 1.4426950408889634
MESH = pl.DeviceIdType.MESH
MASKED = -1e30
K, V, Q, U = 0, 1, 2, 3
PARTNERS = ((0, 1), (1, 0), (3, 0), (1, 1), (3, 1), (2, 0), (2, 1))

NT = (((1,), (1,)), ((), ()))
TN = (((0,), (0,)), ((), ()))


def dot(a, b, dims=(((1,), (0,)), ((), ()))):
    return lax.dot_general(a, b, dims, preferred_element_type=jnp.float32)


def kernel(
    heads_here, blocks, chunk,
    q_hbm, k_hbm, v_hbm, u_hbm, lengths,
    att_ref, dq_ref, dk_ref, dv_ref,
    ks, vs, qs, us, kid, qid, stat_out, stat_in, dk_acc, dv_acc,
    own_sem, sx, rx, sz, rz, ss, rs, ready, odds,
):
    part, blk, me = lax.axis_index("dp"), lax.axis_index("blk"), lax.axis_index("head")
    group = lax.axis_size("head")
    rows = q_hbm.shape[0]
    block = rows * group
    wide = heads_here * HEAD_DIM
    chip, core = me // 2, lax.rem(me, 2)
    chips = group // 2
    after, before = lax.rem(blk + 1, blocks), lax.rem(blk + blocks - 1, blocks)

    def to(dx, dc):
        return lax.rem(chip + dx, chips) * 2 + lax.rem(core + dc, 2)

    def source(dx, dc):
        return lax.rem(chip + chips - dx, chips) * 2 + lax.rem(core + dc, 2)

    inputs = (k_hbm, v_hbm, q_hbm)
    held = (ks, vs, qs)

    def columns(owner, h):
        return pl.ds(pl.multiple_of(owner * wide + h * HEAD_DIM, HEAD_DIM), HEAD_DIM)

    def place(owner, second):
        return pl.ds(pl.multiple_of(owner * rows + second * block, rows), rows)

    def own_half(a):
        return 1 if a in (K, V) else 0

    def neighbour(a):
        return (part, after, me) if a in (K, V) else (part, before, me)

    def x_copy(a, h, dx, dc, owner, target):
        return pltpu.make_async_remote_copy(
            src_ref=inputs[a].at[:, columns(target, h)],
            dst_ref=held[a].at[h, place(owner, own_half(a)), :],
            send_sem=sx.at[a, h],
            recv_sem=rx.at[a, h, dx * 2 + dc],
            device_id=(part, blk, target),
            device_id_type=MESH,
        )

    def z_copy(a, h, owner, src):
        return pltpu.make_async_remote_copy(
            src_ref=src,
            dst_ref=held[a].at[h, place(owner, 1 - own_half(a)), :],
            send_sem=sz.at[a, h],
            recv_sem=rz.at[a, h],
            device_id=neighbour(a),
            device_id_type=MESH,
        )

    def z_all(a, h):
        ref = us if a == U else held[a]
        half = 0 if a in (K, V) else 1
        whole = ref.at[h, half * block : (half + 1) * block, :]
        return pltpu.make_async_remote_copy(
            src_ref=whole, dst_ref=whole, send_sem=sz.at[a, h], recv_sem=rz.at[a, h],
            device_id=neighbour(a), device_id_type=MESH,
        )

    def x_sent(a, h):
        part_of = held[a].at[h, 0 : len(PARTNERS) * rows, :]
        return pltpu.make_async_remote_copy(
            src_ref=part_of, dst_ref=part_of, send_sem=sx.at[a, h], recv_sem=rx.at[a, h, 0],
            device_id=(part, blk, to(0, 1)), device_id_type=MESH,
        )

    own = []
    for h in range(heads_here):
        for a in (K, V, Q):
            own.append(pltpu.make_async_copy(
                inputs[a].at[:, columns(me, h)],
                held[a].at[h, place(me, own_half(a)), :], own_sem.at[a, h]))
        own.append(pltpu.make_async_copy(
            u_hbm.at[:, h * HEAD_DIM : (h + 1) * HEAD_DIM], us.at[h, 0:block, :], own_sem.at[U, h]))
    barrier = pltpu.get_barrier_semaphore()
    for dx, dc in PARTNERS:
        pl.semaphore_signal(barrier, inc=1, device_id=(part, blk, to(dx, dc)), device_id_type=MESH)

    @pl.when(blk > 0)
    def _():
        pl.semaphore_signal(barrier, inc=1, device_id=(part, before, me), device_id_type=MESH)

    for copy in own:
        copy.start()

    spread = 3 * block
    positions = (blk - 1) * block + lax.broadcasted_iota(jnp.int32, (1, spread), 1)
    counted = jnp.zeros((1, spread), jnp.int32)
    end = jnp.int32(0)
    for c in range(lengths.shape[0]):
        end = end + lengths[c]
        counted = counted + jnp.where(positions >= end, 1, 0)
    inside = (positions >= 0) & (positions < blocks * block)
    ids = jnp.where(inside, counted, -1)
    qid[...] = jnp.broadcast_to(ids[:, block:], qid.shape)
    for c in range(2 * block // HEAD_DIM):
        one = jnp.broadcast_to(ids[:, c * HEAD_DIM : (c + 1) * HEAD_DIM], (HEAD_DIM, HEAD_DIM))
        turned = one.T
        for n in range(chunk // HEAD_DIM):
            kid[c * HEAD_DIM : (c + 1) * HEAD_DIM, n * HEAD_DIM : (n + 1) * HEAD_DIM] = turned

    @pl.when(blk == 0)
    def _():
        for h in range(heads_here):
            ks[h, 0:block, :] = jnp.zeros((block, HEAD_DIM), jnp.bfloat16)
            vs[h, 0:block, :] = jnp.zeros((block, HEAD_DIM), jnp.bfloat16)

    pl.semaphore_wait(barrier, len(PARTNERS) + 1 - blk // (blocks - 1))

    has_after, has_before = blk < blocks - 1, blk > 0
    late_before = blk == blocks // 2

    @pl.when(has_after)
    def _():
        pl.semaphore_signal(ready, inc=1, device_id=(part, after, me), device_id_type=MESH)

    def back_up(h):
        pltpu.make_async_remote_copy(
            src_ref=u_hbm.at[:, h * HEAD_DIM : (h + 1) * HEAD_DIM],
            dst_ref=us.at[h, block : 2 * block, :],
            send_sem=sz.at[U, h],
            recv_sem=rz.at[U, h],
            device_id=neighbour(U),
            device_id_type=MESH,
        ).start()

    def own_on(a, h):
        z_copy(a, h, me, inputs[a].at[:, columns(me, h)]).start()

    def on(a, h, owner):
        z_copy(a, h, owner, held[a].at[h, place(owner, own_half(a)), :]).start()

    for h in range(heads_here):
        for a in (K, V):
            for dx, dc in PARTNERS:
                x_copy(a, h, dx, dc, me, to(dx, dc)).start()

            @pl.when(has_after)
            def _():
                own_on(a, h)

        for dx, dc in PARTNERS:
            x_copy(Q, h, dx, dc, me, to(dx, dc)).start()

    early_back = has_before & jnp.logical_not(late_before)

    @pl.when(early_back)
    def _():
        pl.semaphore_wait(ready, 1)
        for h in range(heads_here):
            back_up(h)
            own_on(Q, h)

    for h in range(heads_here):
        for a in (K, V, Q):
            for dx, dc in PARTNERS:
                owner = source(dx, dc)
                x_copy(a, h, dx, dc, owner, me).wait_recv()

                @pl.when(early_back if a == Q else has_after)
                def _():
                    on(a, h, owner)

    @pl.when(late_before)
    def _():
        pl.semaphore_wait(ready, 1)
        for h in range(heads_here):
            back_up(h)
            own_on(Q, h)
            for dx, dc in PARTNERS:
                on(Q, h, source(dx, dc))

    for copy in own:
        copy.wait()

    steps = block // chunk

    def chunk_at(c):
        return pl.ds(pl.multiple_of(c * chunk, chunk), chunk)

    def scores_of(h):
        @pl.when(has_before)
        def _():
            z_all(K, h).wait_recv()

        def step(c, carry):
            at = chunk_at(c)
            same = kid[...] == qid[0:1, at]
            scores = jnp.where(same, dot(ks[h], qs[h, at, :], NT), MASKED)
            top = jnp.max(scores, axis=0, keepdims=True)
            powers = jnp.exp2((scores - top) * (SCALE * LOG2E))
            total = jnp.sum(powers, axis=0, keepdims=True)
            odds[:, at] = powers * (1.0 / total)
            stat_out[h, 0:1, at] = top * (SCALE * LOG2E) + jnp.log2(total)
            return carry

        lax.fori_loop(0, steps, step, 0)

    def output_of(h):
        @pl.when(has_before)
        def _():
            z_all(V, h).wait_recv()

        side = slice(h * HEAD_DIM, (h + 1) * HEAD_DIM)

        def step(c, carry):
            at = chunk_at(c)
            weights = odds[:, at].astype(jnp.bfloat16)
            attended = dot(vs[h], weights, TN).T.astype(jnp.bfloat16)
            att_ref[at, side] = attended
            products = us[h, at, :].astype(jnp.float32) * attended.astype(jnp.float32)
            stat_out[h, 1:2, at] = jnp.sum(products.T, axis=0, keepdims=True)
            return carry

        lax.fori_loop(0, steps, step, 0)

    def grads_of(h):
        side = slice(h * HEAD_DIM, (h + 1) * HEAD_DIM)
        dk_acc[h] = jnp.zeros_like(dk_acc[h])
        dv_acc[h] = jnp.zeros_like(dv_acc[h])

        def step(c, carry):
            at = chunk_at(c)
            query, up = qs[h, at, :], us[h, at, :]
            chances = odds[:, at]
            dscores = (chances * (dot(vs[h], up, NT) - stat_out[h, 1:2, at])).astype(jnp.bfloat16)
            dq_ref[at, side] = (dot(ks[h], dscores, TN) * SCALE).T.astype(jnp.bfloat16)
            dv_acc[h] += dot(odds[block:, at].astype(jnp.bfloat16), up)
            dk_acc[h] += dot(dscores[block:], query)
            return carry

        lax.fori_loop(0, steps, step, 0)

    def stat_copy(h):
        return pltpu.make_async_remote_copy(
            src_ref=stat_out.at[h], dst_ref=stat_in.at[h], send_sem=ss.at[h], recv_sem=rs.at[h],
            device_id=(part, before, me), device_id_type=MESH,
        )

    def cross(h):
        z_all(Q, h).wait_recv()
        z_all(U, h).wait_recv()
        stat_copy(h).wait_recv()

        def step(c, carry):
            at = chunk_at(c)
            there = pl.ds(pl.multiple_of(c * chunk + block, chunk), chunk)
            query, up = qs[h, there, :], us[h, there, :]
            key, value = ks[h, block:, :], vs[h, block:, :]
            same = kid[block:, :] == qid[0:1, there]
            powers = jnp.exp2(dot(key, query, NT) * (SCALE * LOG2E) - stat_in[h, 0:1, at])
            chances = jnp.where(same, powers, 0.0)
            dscores = chances * (dot(value, up, NT) - stat_in[h, 1:2, at])
            dv_acc[h] += dot(chances.astype(jnp.bfloat16), up)
            dk_acc[h] += dot(dscores.astype(jnp.bfloat16), query)
            return carry

        lax.fori_loop(0, steps, step, 0)

    for h in range(heads_here):
        scores_of(h)
        output_of(h)

        @pl.when(has_before)
        def _():
            stat_copy(h).start()

        grads_of(h)

    for h in range(heads_here):

        @pl.when(has_after)
        def _():
            cross(h)

        side = slice(h * HEAD_DIM, (h + 1) * HEAD_DIM)
        dk_ref[:, side] = (dk_acc[h] * SCALE).astype(jnp.bfloat16)
        dv_ref[:, side] = dv_acc[h].astype(jnp.bfloat16)

    for h in range(heads_here):
        for a in (K, V, Q):
            x_sent(a, h).wait_send()

        @pl.when(has_after)
        def _():
            for a in (K, V):
                z_all(a, h).wait_send()

        @pl.when(has_before)
        def _():
            stat_copy(h).wait_send()
            for a in (Q, U):
                z_all(a, h).wait_send()


def store(*refs):
    count = (len(refs) - 1) // 2
    held, outs, sems = refs[:count], refs[count : 2 * count], refs[-1]
    copies = [pltpu.make_async_copy(held[i], outs[i], sems.at[i]) for i in range(count)]
    for copy in copies:
        copy.start()
    for copy in copies:
        copy.wait()


def on_device(queries, key_states, value_states, upstream, clip_lengths):
    block, wide = upstream.shape
    heads_here = wide // HEAD_DIM
    chunk = 256
    group = lax.axis_size("head")
    blocks = lax.axis_size("blk")
    hbm = pl.BlockSpec(memory_space=pl.ANY)
    vmem = pl.BlockSpec(memory_space=pltpu.VMEM)
    out = jax.ShapeDtypeStruct((block, wide), jnp.bfloat16)
    inside = pltpu.VMEM((block, wide), jnp.bfloat16)
    results = pl.pallas_call(
        functools.partial(kernel, heads_here, blocks, chunk),
        out_shape=(inside,) * 4,
        in_specs=[hbm] * 4 + [pl.BlockSpec(memory_space=pltpu.SMEM)],
        out_specs=(vmem,) * 4,
        scratch_shapes=[
            pltpu.VMEM((heads_here, 2 * block, HEAD_DIM), jnp.bfloat16),
            pltpu.VMEM((heads_here, 2 * block, HEAD_DIM), jnp.bfloat16),
            pltpu.VMEM((heads_here, 2 * block, HEAD_DIM), jnp.bfloat16),
            pltpu.VMEM((heads_here, 2 * block, HEAD_DIM), jnp.bfloat16),
            pltpu.VMEM((2 * block, chunk), jnp.int32),
            pltpu.VMEM((8, 2 * block), jnp.int32),
            pltpu.VMEM((heads_here, 8, block), jnp.float32),
            pltpu.VMEM((heads_here, 8, block), jnp.float32),
            pltpu.VMEM((heads_here, block, HEAD_DIM), jnp.float32),
            pltpu.VMEM((heads_here, block, HEAD_DIM), jnp.float32),
            pltpu.SemaphoreType.DMA((4, heads_here)),
            pltpu.SemaphoreType.DMA((3, heads_here)),
            pltpu.SemaphoreType.DMA((3, heads_here, group)),
            pltpu.SemaphoreType.DMA((4, heads_here)),
            pltpu.SemaphoreType.DMA((4, heads_here)),
            pltpu.SemaphoreType.DMA((heads_here,)),
            pltpu.SemaphoreType.DMA((heads_here,)),
            pltpu.SemaphoreType.REGULAR,
            pltpu.VMEM((2 * block, block), jnp.float32),
        ],
        compiler_params=pltpu.CompilerParams(collective_id=0, has_side_effects=True),
    )(queries, key_states, value_states, upstream, clip_lengths)
    return pl.pallas_call(
        store,
        out_shape=(out,) * 4,
        in_specs=[vmem] * 4,
        out_specs=(hbm,) * 4,
        scratch_shapes=[pltpu.SemaphoreType.DMA((4,))],
    )(*[pltpu.with_memory_space_constraint(r, pltpu.VMEM) for r in results])


def solution(mesh):
    return jax.shard_map(
        on_device,
        mesh=mesh,
        in_specs=(
            P(("dp", "blk", "head"), None),
            P(("dp", "blk", "head"), None),
            P(("dp", "blk", "head"), None),
            P(("dp", "blk"), "head"),
            P("dp"),
        ),
        out_specs=(P(("dp", "blk"), "head"),) * 4,
        check_vma=False,
    )
```

```python
import functools

import jax
import jax.numpy as jnp
from jax import lax
from jax.experimental import pallas as pl
from jax.experimental.pallas import tpu as pltpu
from jax.sharding import PartitionSpec as P

HEAD_DIM = 128
SCALE = HEAD_DIM ** (-0.5)
LOG2E = 1.4426950408889634
MESH = pl.DeviceIdType.MESH
MASKED = -1e30
K, V, Q, U = 0, 1, 2, 3
PARTNERS = ((0, 1), (1, 0), (3, 0), (1, 1), (3, 1), (2, 0), (2, 1))

NT = (((1,), (1,)), ((), ()))
TN = (((0,), (0,)), ((), ()))


def dot(a, b, dims=(((1,), (0,)), ((), ()))):
    return lax.dot_general(a, b, dims, preferred_element_type=jnp.float32)


def kernel(
    heads_here, blocks, chunk,
    q_hbm, k_hbm, v_hbm, u_hbm, lengths,
    att_ref, dq_ref, dk_ref, dv_ref,
    ks, vs, qs, us, kid, qid, stat_out, stat_in, dk_acc, dv_acc,
    own_sem, sx, rx, sz, rz, ss, rs, ready, led, rr, odds,
):
    part, blk, me = lax.axis_index("dp"), lax.axis_index("blk"), lax.axis_index("head")
    group = lax.axis_size("head")
    rows = q_hbm.shape[0]
    block = rows * group
    wide = heads_here * HEAD_DIM
    chip, core = me // 2, lax.rem(me, 2)
    chips = group // 2
    after, before = lax.rem(blk + 1, blocks), lax.rem(blk + blocks - 1, blocks)

    def to(dx, dc):
        return lax.rem(chip + dx, chips) * 2 + lax.rem(core + dc, 2)

    def source(dx, dc):
        return lax.rem(chip + chips - dx, chips) * 2 + lax.rem(core + dc, 2)

    inputs = (k_hbm, v_hbm, q_hbm)
    held = (ks, vs, qs)

    def columns(owner, h):
        return pl.ds(pl.multiple_of(owner * wide + h * HEAD_DIM, HEAD_DIM), HEAD_DIM)

    def place(owner, second):
        return pl.ds(pl.multiple_of(owner * rows + second * block, rows), rows)

    def own_half(a):
        return 1 if a in (K, V) else 0

    def neighbour(a):
        return (part, after, me) if a in (K, V) else (part, before, me)

    def x_copy(a, h, dx, dc, owner, target):
        return x_at(a, h, dx * 2 + dc, owner, target)

    def x_at(a, h, slot, owner, target):
        return pltpu.make_async_remote_copy(
            src_ref=inputs[a].at[:, columns(target, h)],
            dst_ref=held[a].at[h, place(owner, own_half(a)), :],
            send_sem=sx.at[a, h],
            recv_sem=rx.at[a, h, slot],
            device_id=(part, blk, target),
            device_id_type=MESH,
        )

    def z_copy(a, h, owner, src):
        return pltpu.make_async_remote_copy(
            src_ref=src,
            dst_ref=held[a].at[h, place(owner, 1 - own_half(a)), :],
            send_sem=sz.at[a, h],
            recv_sem=rz.at[a, h],
            device_id=neighbour(a),
            device_id_type=MESH,
        )

    def z_all(a, h):
        ref = us if a == U else held[a]
        half = 0 if a in (K, V) else 1
        whole = ref.at[h, half * block : (half + 1) * block, :]
        return pltpu.make_async_remote_copy(
            src_ref=whole, dst_ref=whole, send_sem=sz.at[a, h], recv_sem=rz.at[a, h],
            device_id=neighbour(a), device_id_type=MESH,
        )

    def x_sent(a, h):
        part_of = held[a].at[h, 0 : len(PARTNERS) * rows, :]
        return pltpu.make_async_remote_copy(
            src_ref=part_of, dst_ref=part_of, send_sem=sx.at[a, h], recv_sem=rx.at[a, h, 0],
            device_id=(part, blk, to(0, 1)), device_id_type=MESH,
        )

    own = []
    for h in range(heads_here):
        for a in (K, V, Q):
            own.append(pltpu.make_async_copy(
                inputs[a].at[:, columns(me, h)],
                held[a].at[h, place(me, own_half(a)), :], own_sem.at[a, h]))
        own.append(pltpu.make_async_copy(
            u_hbm.at[:, h * HEAD_DIM : (h + 1) * HEAD_DIM], us.at[h, 0:block, :], own_sem.at[U, h]))
    has_after, has_before = blk < blocks - 1, blk > 0
    half, last = blocks // 2, blocks - 1
    late_before = blk == half
    leads_half, relays = blk == half - 1, blk == last
    late_group = (part == 0) & (blk == 0)
    leader, member = late_group & (me == 0), late_group & (me > 0)

    barrier = pltpu.get_barrier_semaphore()

    @pl.when(jnp.logical_not(leader))
    def _():
        for dx, dc in PARTNERS:
            pl.semaphore_signal(barrier, inc=1, device_id=(part, blk, to(dx, dc)), device_id_type=MESH)

    @pl.when(has_before)
    def _():
        pl.semaphore_signal(barrier, inc=1, device_id=(part, before, me), device_id_type=MESH)

    @pl.when(late_before)
    def _():
        pl.semaphore_signal(barrier, inc=1, device_id=(part, last, me), device_id_type=MESH)

    @pl.when(relays)
    def _():
        pl.semaphore_signal(barrier, inc=1, device_id=(part, half - 1, me), device_id_type=MESH)

    for copy in own:
        copy.start()

    def back_up(h):
        pltpu.make_async_remote_copy(
            src_ref=u_hbm.at[:, h * HEAD_DIM : (h + 1) * HEAD_DIM],
            dst_ref=us.at[h, block : 2 * block, :],
            send_sem=sz.at[U, h],
            recv_sem=rz.at[U, h],
            device_id=neighbour(U),
            device_id_type=MESH,
        ).start()

    def relay_in(h, owner, src):
        return pltpu.make_async_remote_copy(
            src_ref=src,
            dst_ref=us.at[h, place(owner, 1), :],
            send_sem=sz.at[V, h],
            recv_sem=rr.at[h, owner],
            device_id=(part, last, me),
            device_id_type=MESH,
        )

    def relay_out(h, owner):
        return pltpu.make_async_remote_copy(
            src_ref=us.at[h, place(owner, 1), :],
            dst_ref=vs.at[h, place(owner, 0), :],
            send_sem=sz.at[V, h],
            recv_sem=rz.at[V, h],
            device_id=(part, half, me),
            device_id_type=MESH,
        )

    def at_home(a, h, owner):
        return held[a].at[h, place(owner, own_half(a)), :]

    def own_rows(a, h):
        return inputs[a].at[:, columns(me, h)]

    order = [(a, h) for h in range(heads_here) for a in (K, V)] + [(Q, h) for h in range(heads_here)]

    def prepare():
        spread = 3 * block
        positions = (blk - 1) * block + lax.broadcasted_iota(jnp.int32, (1, spread), 1)
        counted = jnp.zeros((1, spread), jnp.int32)
        end = jnp.int32(0)
        for c in range(lengths.shape[0]):
            end = end + lengths[c]
            counted = counted + jnp.where(positions >= end, 1, 0)
        inside = (positions >= 0) & (positions < blocks * block)
        ids = jnp.where(inside, counted, -1)
        qid[...] = jnp.broadcast_to(ids[:, block:], qid.shape)
        for c in range(2 * block // HEAD_DIM):
            one = jnp.broadcast_to(ids[:, c * HEAD_DIM : (c + 1) * HEAD_DIM], (HEAD_DIM, HEAD_DIM))
            turned = one.T
            for n in range(chunk // HEAD_DIM):
                kid[c * HEAD_DIM : (c + 1) * HEAD_DIM, n * HEAD_DIM : (n + 1) * HEAD_DIM] = turned

        @pl.when(blk == 0)
        def _():
            for h in range(heads_here):
                ks[h, 0:block, :] = jnp.zeros((block, HEAD_DIM), jnp.bfloat16)
                vs[h, 0:block, :] = jnp.zeros((block, HEAD_DIM), jnp.bfloat16)

        for h in range(heads_here):
            dk_acc[h] = jnp.zeros_like(dk_acc[h])
            dv_acc[h] = jnp.zeros_like(dv_acc[h])

    def traffic(peers, to_after, to_before, aside=False, relay=False, late=False, wait_leader=False):
        pl.semaphore_wait(barrier, peers)

        if to_after and not to_before and not wait_leader:

            @pl.when(leader)
            def _():
                for dx, dc in PARTNERS:
                    pl.semaphore_signal(led, inc=1, device_id=(part, blk, to(dx, dc)), device_id_type=MESH)

        if to_after:
            pl.semaphore_signal(ready, inc=1, device_id=(part, after, me), device_id_type=MESH)

        def pass_on(a, h, owner, src):
            if a == Q:
                if to_before and not late:
                    z_copy(a, h, owner, src).start()
            elif to_after:
                if aside and a == V:
                    relay_in(h, owner, src).start()
                else:
                    z_copy(a, h, owner, src).start()

        def start(a, h, dx, dc):
            if wait_leader:

                @pl.when(to(dx, dc) != 0)
                def _():
                    x_copy(a, h, dx, dc, me, to(dx, dc)).start()
            else:
                x_copy(a, h, dx, dc, me, to(dx, dc)).start()

        def take(a, h, dx, dc):
            owner = source(dx, dc)

            def now():
                x_copy(a, h, dx, dc, owner, me).wait_recv()
                pass_on(a, h, owner, at_home(a, h, owner))

            if wait_leader:
                pl.when(owner != 0)(now)
            else:
                now()

        def send_back():
            pl.semaphore_wait(ready, 1)
            for h in range(heads_here):
                back_up(h)
                z_copy(Q, h, me, own_rows(Q, h)).start()

        def send(a, h):
            if a != Q:
                pass_on(a, h, me, own_rows(a, h))
            for dx, dc in PARTNERS:
                start(a, h, dx, dc)

        for a, h in order:
            send(a, h)
        if to_before and not late:
            send_back()
        prepare()
        for a, h in order:
            for dx, dc in PARTNERS:
                take(a, h, dx, dc)
            if relay and a == V:
                for owner in range(group):
                    relay_in(h, owner, us.at[h, place(owner, 1), :]).wait_recv()
                    relay_out(h, owner).start()
        if wait_leader:
            pl.semaphore_wait(led, 1)
            back = lax.rem(chips - chip, chips) * 2 + core
            for a, h in order:
                x_at(a, h, back, me, 0).start()
            for a, h in order:
                x_at(a, h, me, 0, me).wait_recv()
                pass_on(a, h, 0, at_home(a, h, 0))
        if late:
            send_back()
            for h in range(heads_here):
                for dx, dc in PARTNERS:
                    owner = source(dx, dc)
                    z_copy(Q, h, owner, at_home(Q, h, owner)).start()

    @pl.when(has_before & has_after & (blk != half - 1) & (blk != half))
    def _():
        traffic(len(PARTNERS) + 1, True, True)

    @pl.when((blk == 0) & jnp.logical_not(member))
    def _():
        traffic(len(PARTNERS) + 1, True, False)

    @pl.when(member)
    def _():
        traffic(len(PARTNERS), True, False, wait_leader=True)

    @pl.when(leads_half)
    def _():
        traffic(len(PARTNERS) + 2, True, True, aside=True)

    @pl.when(late_before)
    def _():
        traffic(len(PARTNERS) + 1, True, True, late=True)

    @pl.when(relays)
    def _():
        traffic(len(PARTNERS) + 1, False, True, relay=True)

    for copy in own:
        copy.wait()

    steps = block // chunk

    def chunk_at(c):
        return pl.ds(pl.multiple_of(c * chunk, chunk), chunk)

    def scores_of(h):
        @pl.when(has_before)
        def _():
            z_all(K, h).wait_recv()

        def step(c, carry):
            at = chunk_at(c)
            same = kid[...] == qid[0:1, at]
            scores = jnp.where(same, dot(ks[h], qs[h, at, :], NT), MASKED)
            top = jnp.max(scores, axis=0, keepdims=True)
            powers = jnp.exp2((scores - top) * (SCALE * LOG2E))
            total = jnp.sum(powers, axis=0, keepdims=True)
            odds[:, at] = powers * (1.0 / total)
            stat_out[h, 0:1, at] = top * (SCALE * LOG2E) + jnp.log2(total)
            return carry

        lax.fori_loop(0, steps, step, 0)

    def output_of(h):
        @pl.when(has_before)
        def _():
            z_all(V, h).wait_recv()

        side = slice(h * HEAD_DIM, (h + 1) * HEAD_DIM)

        def step(c, carry):
            at = chunk_at(c)
            weights = odds[:, at].astype(jnp.bfloat16)
            attended = dot(vs[h], weights, TN).T.astype(jnp.bfloat16)
            att_ref[at, side] = attended
            products = us[h, at, :].astype(jnp.float32) * attended.astype(jnp.float32)
            stat_out[h, 1:2, at] = jnp.sum(products.T, axis=0, keepdims=True)
            return carry

        lax.fori_loop(0, steps, step, 0)

    def grads_of(h):
        side = slice(h * HEAD_DIM, (h + 1) * HEAD_DIM)

        def step(c, carry):
            at = chunk_at(c)
            query, up = qs[h, at, :], us[h, at, :]
            chances = odds[:, at]
            dscores = (chances * (dot(vs[h], up, NT) - stat_out[h, 1:2, at])).astype(jnp.bfloat16)
            dq_ref[at, side] = (dot(ks[h], dscores, TN) * SCALE).T.astype(jnp.bfloat16)
            dv_acc[h] += dot(odds[block:, at].astype(jnp.bfloat16), up)
            dk_acc[h] += dot(dscores[block:], query)
            return carry

        lax.fori_loop(0, steps, step, 0)

    def stat_copy(h):
        return pltpu.make_async_remote_copy(
            src_ref=stat_out.at[h], dst_ref=stat_in.at[h], send_sem=ss.at[h], recv_sem=rs.at[h],
            device_id=(part, before, me), device_id_type=MESH,
        )

    def cross(h):
        z_all(Q, h).wait_recv()
        z_all(U, h).wait_recv()
        stat_copy(h).wait_recv()

        def step(c, carry):
            at = chunk_at(c)
            there = pl.ds(pl.multiple_of(c * chunk + block, chunk), chunk)
            query, up = qs[h, there, :], us[h, there, :]
            key, value = ks[h, block:, :], vs[h, block:, :]
            same = kid[block:, :] == qid[0:1, there]
            powers = jnp.exp2(dot(key, query, NT) * (SCALE * LOG2E) - stat_in[h, 0:1, at])
            chances = jnp.where(same, powers, 0.0)
            dscores = chances * (dot(value, up, NT) - stat_in[h, 1:2, at])
            dv_acc[h] += dot(chances.astype(jnp.bfloat16), up)
            dk_acc[h] += dot(dscores.astype(jnp.bfloat16), query)
            return carry

        lax.fori_loop(0, steps, step, 0)

    cross_first = late_before | ((part == 0) & (blk == 1))
    cross_later = has_after & jnp.logical_not(cross_first)

    @pl.when(cross_first)
    def _():
        for h in range(heads_here):
            cross(h)

    for h in range(heads_here):
        scores_of(h)
        output_of(h)

        @pl.when(has_before)
        def _():
            stat_copy(h).start()

        grads_of(h)

    @pl.when(cross_later)
    def _():
        for h in range(heads_here):
            cross(h)

    for h in range(heads_here):
        side = slice(h * HEAD_DIM, (h + 1) * HEAD_DIM)
        dk_ref[:, side] = (dk_acc[h] * SCALE).astype(jnp.bfloat16)
        dv_ref[:, side] = dv_acc[h].astype(jnp.bfloat16)

    for h in range(heads_here):
        for a in (K, V, Q):
            x_sent(a, h).wait_send()

        @pl.when(has_after)
        def _():
            z_all(K, h).wait_send()

        @pl.when(has_after | relays)
        def _():
            z_all(V, h).wait_send()

        @pl.when(has_before)
        def _():
            stat_copy(h).wait_send()
            for a in (Q, U):
                z_all(a, h).wait_send()


def store(*refs):
    count = (len(refs) - 1) // 2
    held, outs, sems = refs[:count], refs[count : 2 * count], refs[-1]
    copies = [pltpu.make_async_copy(held[i], outs[i], sems.at[i]) for i in range(count)]
    for copy in copies:
        copy.start()
    for copy in copies:
        copy.wait()


def on_device(queries, key_states, value_states, upstream, clip_lengths):
    block, wide = upstream.shape
    heads_here = wide // HEAD_DIM
    chunk = 512
    group = lax.axis_size("head")
    blocks = lax.axis_size("blk")
    hbm = pl.BlockSpec(memory_space=pl.ANY)
    vmem = pl.BlockSpec(memory_space=pltpu.VMEM)
    out = jax.ShapeDtypeStruct((block, wide), jnp.bfloat16)
    inside = pltpu.VMEM((block, wide), jnp.bfloat16)
    results = pl.pallas_call(
        functools.partial(kernel, heads_here, blocks, chunk),
        out_shape=(inside,) * 4,
        in_specs=[hbm] * 4 + [pl.BlockSpec(memory_space=pltpu.SMEM)],
        out_specs=(vmem,) * 4,
        scratch_shapes=[
            pltpu.VMEM((heads_here, 2 * block, HEAD_DIM), jnp.bfloat16),
            pltpu.VMEM((heads_here, 2 * block, HEAD_DIM), jnp.bfloat16),
            pltpu.VMEM((heads_here, 2 * block, HEAD_DIM), jnp.bfloat16),
            pltpu.VMEM((heads_here, 2 * block, HEAD_DIM), jnp.bfloat16),
            pltpu.VMEM((2 * block, chunk), jnp.int32),
            pltpu.VMEM((8, 2 * block), jnp.int32),
            pltpu.VMEM((heads_here, 8, block), jnp.float32),
            pltpu.VMEM((heads_here, 8, block), jnp.float32),
            pltpu.VMEM((heads_here, block, HEAD_DIM), jnp.float32),
            pltpu.VMEM((heads_here, block, HEAD_DIM), jnp.float32),
            pltpu.SemaphoreType.DMA((4, heads_here)),
            pltpu.SemaphoreType.DMA((3, heads_here)),
            pltpu.SemaphoreType.DMA((3, heads_here, group)),
            pltpu.SemaphoreType.DMA((4, heads_here)),
            pltpu.SemaphoreType.DMA((4, heads_here)),
            pltpu.SemaphoreType.DMA((heads_here,)),
            pltpu.SemaphoreType.DMA((heads_here,)),
            pltpu.SemaphoreType.REGULAR,
            pltpu.SemaphoreType.REGULAR,
            pltpu.SemaphoreType.DMA((heads_here, group)),
            pltpu.VMEM((2 * block, block), jnp.float32),
        ],
        compiler_params=pltpu.CompilerParams(collective_id=0, has_side_effects=True),
    )(queries, key_states, value_states, upstream, clip_lengths)
    return pl.pallas_call(
        store,
        out_shape=(out,) * 4,
        in_specs=[vmem] * 4,
        out_specs=(hbm,) * 4,
        scratch_shapes=[pltpu.SemaphoreType.DMA((4,))],
    )(*[pltpu.with_memory_space_constraint(r, pltpu.VMEM) for r in results])


def solution(mesh):
    return jax.shard_map(
        on_device,
        mesh=mesh,
        in_specs=(
            P(("dp", "blk", "head"), None),
            P(("dp", "blk", "head"), None),
            P(("dp", "blk", "head"), None),
            P(("dp", "blk"), "head"),
            P("dp"),
        ),
        out_specs=(P(("dp", "blk"), "head"),) * 4,
        check_vma=False,
    )
```

```python
import functools

import jax
import jax.numpy as jnp
from jax import lax
from jax.experimental import pallas as pl
from jax.experimental.pallas import tpu as pltpu
from jax.sharding import PartitionSpec as P

HEAD_DIM = 128
SCALE = HEAD_DIM ** (-0.5)
LOG2E = 1.4426950408889634
MESH = pl.DeviceIdType.MESH
MASKED = -1e30
K, V, Q, U = 0, 1, 2, 3
PARTNERS = ((0, 1), (1, 0), (3, 0), (1, 1), (3, 1), (2, 0), (2, 1))

NT = (((1,), (1,)), ((), ()))
TN = (((0,), (0,)), ((), ()))


def dot(a, b, dims=(((1,), (0,)), ((), ()))):
    return lax.dot_general(a, b, dims, preferred_element_type=jnp.float32)


def kernel(
    heads_here, blocks, chunk,
    q_hbm, k_hbm, v_hbm, u_hbm, lengths,
    att_ref, dq_ref, dk_ref, dv_ref,
    ks, vs, qs, us, kid, qid, stat_out, stat_in, dk_acc, dv_acc,
    own_sem, sx, rx, sz, rz, ss, rs, ready, led, rr, odds,
):
    part, blk, me = lax.axis_index("dp"), lax.axis_index("blk"), lax.axis_index("head")
    group = lax.axis_size("head")
    rows = q_hbm.shape[0]
    block = rows * group
    wide = heads_here * HEAD_DIM
    chip, core = me // 2, lax.rem(me, 2)
    chips = group // 2
    after, before = lax.rem(blk + 1, blocks), lax.rem(blk + blocks - 1, blocks)

    def to(dx, dc):
        return lax.rem(chip + dx, chips) * 2 + lax.rem(core + dc, 2)

    def source(dx, dc):
        return lax.rem(chip + chips - dx, chips) * 2 + lax.rem(core + dc, 2)

    inputs = (k_hbm, v_hbm, q_hbm)
    held = (ks, vs, qs)

    def columns(owner, h):
        return pl.ds(pl.multiple_of(owner * wide + h * HEAD_DIM, HEAD_DIM), HEAD_DIM)

    def place(owner, second):
        return pl.ds(pl.multiple_of(owner * rows + second * block, rows), rows)

    def own_half(a):
        return 1 if a in (K, V) else 0

    def neighbour(a):
        return (part, after, me) if a in (K, V) else (part, before, me)

    def x_copy(a, h, dx, dc, owner, target):
        return x_at(a, h, dx * 2 + dc, owner, target)

    def x_at(a, h, slot, owner, target):
        return pltpu.make_async_remote_copy(
            src_ref=inputs[a].at[:, columns(target, h)],
            dst_ref=held[a].at[h, place(owner, own_half(a)), :],
            send_sem=sx.at[a, h],
            recv_sem=rx.at[a, h, slot],
            device_id=(part, blk, target),
            device_id_type=MESH,
        )

    def z_copy(a, h, owner, src):
        return pltpu.make_async_remote_copy(
            src_ref=src,
            dst_ref=held[a].at[h, place(owner, 1 - own_half(a)), :],
            send_sem=sz.at[a, h],
            recv_sem=rz.at[a, h],
            device_id=neighbour(a),
            device_id_type=MESH,
        )

    def z_all(a, h):
        ref = us if a == U else held[a]
        half = 0 if a in (K, V) else 1
        whole = ref.at[h, half * block : (half + 1) * block, :]
        return pltpu.make_async_remote_copy(
            src_ref=whole, dst_ref=whole, send_sem=sz.at[a, h], recv_sem=rz.at[a, h],
            device_id=neighbour(a), device_id_type=MESH,
        )

    def x_sent(a, h):
        part_of = held[a].at[h, 0 : len(PARTNERS) * rows, :]
        return pltpu.make_async_remote_copy(
            src_ref=part_of, dst_ref=part_of, send_sem=sx.at[a, h], recv_sem=rx.at[a, h, 0],
            device_id=(part, blk, to(0, 1)), device_id_type=MESH,
        )

    own = []
    for h in range(heads_here):
        for a in (K, V, Q):
            own.append(pltpu.make_async_copy(
                inputs[a].at[:, columns(me, h)],
                held[a].at[h, place(me, own_half(a)), :], own_sem.at[a, h]))
        own.append(pltpu.make_async_copy(
            u_hbm.at[:, h * HEAD_DIM : (h + 1) * HEAD_DIM], us.at[h, 0:block, :], own_sem.at[U, h]))
    has_after, has_before = blk < blocks - 1, blk > 0
    half, last = blocks // 2, blocks - 1
    late_before = blk == half
    leads_half, relays = blk == half - 1, blk == last
    late_group = (part == 0) & (blk == 0)
    leader, member = late_group & (me == 0), late_group & (me > 0)

    barrier = pltpu.get_barrier_semaphore()

    @pl.when(jnp.logical_not(leader))
    def _():
        for dx, dc in PARTNERS:
            pl.semaphore_signal(barrier, inc=1, device_id=(part, blk, to(dx, dc)), device_id_type=MESH)

    @pl.when(has_before)
    def _():
        pl.semaphore_signal(barrier, inc=1, device_id=(part, before, me), device_id_type=MESH)

    @pl.when(late_before)
    def _():
        pl.semaphore_signal(barrier, inc=1, device_id=(part, last, me), device_id_type=MESH)

    @pl.when(relays)
    def _():
        pl.semaphore_signal(barrier, inc=1, device_id=(part, half - 1, me), device_id_type=MESH)

    for copy in own:
        copy.start()

    def back_up(h):
        pltpu.make_async_remote_copy(
            src_ref=u_hbm.at[:, h * HEAD_DIM : (h + 1) * HEAD_DIM],
            dst_ref=us.at[h, block : 2 * block, :],
            send_sem=sz.at[U, h],
            recv_sem=rz.at[U, h],
            device_id=neighbour(U),
            device_id_type=MESH,
        ).start()

    def relay_in(h, owner, src):
        return pltpu.make_async_remote_copy(
            src_ref=src,
            dst_ref=us.at[h, place(owner, 1), :],
            send_sem=sz.at[V, h],
            recv_sem=rr.at[h, owner],
            device_id=(part, last, me),
            device_id_type=MESH,
        )

    def relay_out(h, owner):
        return pltpu.make_async_remote_copy(
            src_ref=us.at[h, place(owner, 1), :],
            dst_ref=vs.at[h, place(owner, 0), :],
            send_sem=sz.at[V, h],
            recv_sem=rz.at[V, h],
            device_id=(part, half, me),
            device_id_type=MESH,
        )

    def at_home(a, h, owner):
        return held[a].at[h, place(owner, own_half(a)), :]

    def own_rows(a, h):
        return inputs[a].at[:, columns(me, h)]

    order = [(a, h) for h in range(heads_here) for a in (K, V)] + [(Q, h) for h in range(heads_here)]

    def prepare():
        spread = 3 * block
        positions = (blk - 1) * block + lax.broadcasted_iota(jnp.int32, (1, spread), 1)
        counted = jnp.zeros((1, spread), jnp.int32)
        end = jnp.int32(0)
        for c in range(lengths.shape[0]):
            end = end + lengths[c]
            counted = counted + jnp.where(positions >= end, 1, 0)
        inside = (positions >= 0) & (positions < blocks * block)
        ids = jnp.where(inside, counted, -1)
        qid[...] = jnp.broadcast_to(ids[:, block:], qid.shape)
        for c in range(2 * block // HEAD_DIM):
            one = jnp.broadcast_to(ids[:, c * HEAD_DIM : (c + 1) * HEAD_DIM], (HEAD_DIM, HEAD_DIM))
            turned = one.T
            for n in range(chunk // HEAD_DIM):
                kid[c * HEAD_DIM : (c + 1) * HEAD_DIM, n * HEAD_DIM : (n + 1) * HEAD_DIM] = turned

        @pl.when(blk == 0)
        def _():
            for h in range(heads_here):
                ks[h, 0:block, :] = jnp.zeros((block, HEAD_DIM), jnp.bfloat16)
                vs[h, 0:block, :] = jnp.zeros((block, HEAD_DIM), jnp.bfloat16)

        for h in range(heads_here):
            dk_acc[h] = jnp.zeros_like(dk_acc[h])
            dv_acc[h] = jnp.zeros_like(dv_acc[h])

    def traffic(peers, to_after, to_before, aside=False, relay=False, late=False, wait_leader=False):
        pl.semaphore_wait(barrier, peers)

        if to_after and not to_before and not wait_leader:

            @pl.when(leader)
            def _():
                for dx, dc in PARTNERS:
                    pl.semaphore_signal(led, inc=1, device_id=(part, blk, to(dx, dc)), device_id_type=MESH)

        if to_after:
            pl.semaphore_signal(ready, inc=1, device_id=(part, after, me), device_id_type=MESH)

        def pass_on(a, h, owner, src):
            if a == Q:
                if to_before and not late:
                    z_copy(a, h, owner, src).start()
            elif to_after:
                if aside and a == V:
                    relay_in(h, owner, src).start()
                else:
                    z_copy(a, h, owner, src).start()

        def start(a, h, dx, dc):
            if wait_leader:

                @pl.when(to(dx, dc) != 0)
                def _():
                    x_copy(a, h, dx, dc, me, to(dx, dc)).start()
            else:
                x_copy(a, h, dx, dc, me, to(dx, dc)).start()

        def take(a, h, dx, dc):
            owner = source(dx, dc)

            def now():
                x_copy(a, h, dx, dc, owner, me).wait_recv()
                pass_on(a, h, owner, at_home(a, h, owner))

            if wait_leader:
                pl.when(owner != 0)(now)
            else:
                now()

        def send_back():
            pl.semaphore_wait(ready, 1)
            for h in range(heads_here):
                back_up(h)
                z_copy(Q, h, me, own_rows(Q, h)).start()

        def send(a, h):
            if a != Q:
                pass_on(a, h, me, own_rows(a, h))
            for dx, dc in PARTNERS:
                start(a, h, dx, dc)

        for a, h in order:
            send(a, h)
        if to_before and not late:
            send_back()
        prepare()
        for a, h in order:
            for dx, dc in PARTNERS:
                take(a, h, dx, dc)
            if relay and a == V:
                for owner in [me] + [source(dx, dc) for dx, dc in PARTNERS]:
                    relay_in(h, owner, us.at[h, place(owner, 1), :]).wait_recv()
                    relay_out(h, owner).start()
        if wait_leader:
            pl.semaphore_wait(led, 1)
            back = lax.rem(chips - chip, chips) * 2 + core
            for a, h in order:
                x_at(a, h, back, me, 0).start()
            for a, h in order:
                x_at(a, h, me, 0, me).wait_recv()
                pass_on(a, h, 0, at_home(a, h, 0))
        if late:
            send_back()
            for h in range(heads_here):
                for dx, dc in PARTNERS:
                    owner = source(dx, dc)
                    z_copy(Q, h, owner, at_home(Q, h, owner)).start()

    @pl.when(has_before & has_after & (blk != half - 1) & (blk != half))
    def _():
        traffic(len(PARTNERS) + 1, True, True)

    @pl.when((blk == 0) & jnp.logical_not(member))
    def _():
        traffic(len(PARTNERS) + 1, True, False)

    @pl.when(member)
    def _():
        traffic(len(PARTNERS), True, False, wait_leader=True)

    @pl.when(leads_half)
    def _():
        traffic(len(PARTNERS) + 2, True, True, aside=True)

    @pl.when(late_before)
    def _():
        traffic(len(PARTNERS) + 1, True, True, late=True)

    @pl.when(relays)
    def _():
        traffic(len(PARTNERS) + 1, False, True, relay=True)

    for copy in own:
        copy.wait()

    steps = block // chunk

    def chunk_at(c):
        return pl.ds(pl.multiple_of(c * chunk, chunk), chunk)

    def scores_of(h):
        @pl.when(has_before)
        def _():
            z_all(K, h).wait_recv()

        def step(c, carry):
            at = chunk_at(c)
            same = kid[...] == qid[0:1, at]
            scores = jnp.where(same, dot(ks[h], qs[h, at, :], NT), MASKED)
            top = jnp.max(scores, axis=0, keepdims=True)
            powers = jnp.exp2((scores - top) * (SCALE * LOG2E))
            total = jnp.sum(powers, axis=0, keepdims=True)
            odds[:, at] = powers * (1.0 / total)
            stat_out[h, 0:1, at] = top * (SCALE * LOG2E) + jnp.log2(total)
            return carry

        lax.fori_loop(0, steps, step, 0)

    def output_of(h):
        @pl.when(has_before)
        def _():
            z_all(V, h).wait_recv()

        side = slice(h * HEAD_DIM, (h + 1) * HEAD_DIM)

        def step(c, carry):
            at = chunk_at(c)
            weights = odds[:, at].astype(jnp.bfloat16)
            attended = dot(vs[h], weights, TN).T.astype(jnp.bfloat16)
            att_ref[at, side] = attended
            products = us[h, at, :].astype(jnp.float32) * attended.astype(jnp.float32)
            stat_out[h, 1:2, at] = jnp.sum(products.T, axis=0, keepdims=True)
            return carry

        lax.fori_loop(0, steps, step, 0)

    def grads_of(h):
        side = slice(h * HEAD_DIM, (h + 1) * HEAD_DIM)

        def step(c, carry):
            at = chunk_at(c)
            query, up = qs[h, at, :], us[h, at, :]
            chances = odds[:, at]
            dscores = (chances * (dot(vs[h], up, NT) - stat_out[h, 1:2, at])).astype(jnp.bfloat16)
            dq_ref[at, side] = (dot(ks[h], dscores, TN) * SCALE).T.astype(jnp.bfloat16)
            dv_acc[h] += dot(odds[block:, at].astype(jnp.bfloat16), up)
            dk_acc[h] += dot(dscores[block:], query)
            return carry

        lax.fori_loop(0, steps, step, 0)

    def stat_copy(h):
        return pltpu.make_async_remote_copy(
            src_ref=stat_out.at[h], dst_ref=stat_in.at[h], send_sem=ss.at[h], recv_sem=rs.at[h],
            device_id=(part, before, me), device_id_type=MESH,
        )

    def cross(h):
        z_all(Q, h).wait_recv()
        z_all(U, h).wait_recv()
        stat_copy(h).wait_recv()

        def step(c, carry):
            at = chunk_at(c)
            there = pl.ds(pl.multiple_of(c * chunk + block, chunk), chunk)
            query, up = qs[h, there, :], us[h, there, :]
            key, value = ks[h, block:, :], vs[h, block:, :]
            same = kid[block:, :] == qid[0:1, there]
            powers = jnp.exp2(dot(key, query, NT) * (SCALE * LOG2E) - stat_in[h, 0:1, at])
            chances = jnp.where(same, powers, 0.0)
            dscores = chances * (dot(value, up, NT) - stat_in[h, 1:2, at])
            dv_acc[h] += dot(chances.astype(jnp.bfloat16), up)
            dk_acc[h] += dot(dscores.astype(jnp.bfloat16), query)
            return carry

        lax.fori_loop(0, steps, step, 0)

    cross_first = late_before | ((part == 0) & (blk == 1))
    cross_later = has_after & jnp.logical_not(cross_first)

    @pl.when(cross_first)
    def _():
        for h in range(heads_here):
            cross(h)

    for h in range(heads_here):
        scores_of(h)
        output_of(h)

        @pl.when(has_before)
        def _():
            stat_copy(h).start()

        grads_of(h)

    @pl.when(cross_later)
    def _():
        for h in range(heads_here):
            cross(h)

    for h in range(heads_here):
        side = slice(h * HEAD_DIM, (h + 1) * HEAD_DIM)
        dk_ref[:, side] = (dk_acc[h] * SCALE).astype(jnp.bfloat16)
        dv_ref[:, side] = dv_acc[h].astype(jnp.bfloat16)

    for h in range(heads_here):
        for a in (K, V, Q):
            x_sent(a, h).wait_send()

        @pl.when(has_after)
        def _():
            z_all(K, h).wait_send()

        @pl.when(has_after | relays)
        def _():
            z_all(V, h).wait_send()

        @pl.when(has_before)
        def _():
            stat_copy(h).wait_send()
            for a in (Q, U):
                z_all(a, h).wait_send()


def store(*refs):
    count = (len(refs) - 1) // 2
    held, outs, sems = refs[:count], refs[count : 2 * count], refs[-1]
    rows = held[0].shape[0] // 2
    copies = [
        pltpu.make_async_copy(
            held[i].at[n * rows : (n + 1) * rows], outs[i].at[n * rows : (n + 1) * rows], sems.at[i, n]
        )
        for i in range(count)
        for n in range(2)
    ]
    for copy in copies:
        copy.start()
    for copy in copies:
        copy.wait()


def on_device(queries, key_states, value_states, upstream, clip_lengths):
    block, wide = upstream.shape
    heads_here = wide // HEAD_DIM
    chunk = 512
    group = lax.axis_size("head")
    blocks = lax.axis_size("blk")
    hbm = pl.BlockSpec(memory_space=pl.ANY)
    vmem = pl.BlockSpec(memory_space=pltpu.VMEM)
    out = jax.ShapeDtypeStruct((block, wide), jnp.bfloat16)
    inside = pltpu.VMEM((block, wide), jnp.bfloat16)
    results = pl.pallas_call(
        functools.partial(kernel, heads_here, blocks, chunk),
        out_shape=(inside,) * 4,
        in_specs=[hbm] * 4 + [pl.BlockSpec(memory_space=pltpu.SMEM)],
        out_specs=(vmem,) * 4,
        scratch_shapes=[
            pltpu.VMEM((heads_here, 2 * block, HEAD_DIM), jnp.bfloat16),
            pltpu.VMEM((heads_here, 2 * block, HEAD_DIM), jnp.bfloat16),
            pltpu.VMEM((heads_here, 2 * block, HEAD_DIM), jnp.bfloat16),
            pltpu.VMEM((heads_here, 2 * block, HEAD_DIM), jnp.bfloat16),
            pltpu.VMEM((2 * block, chunk), jnp.int32),
            pltpu.VMEM((8, 2 * block), jnp.int32),
            pltpu.VMEM((heads_here, 8, block), jnp.float32),
            pltpu.VMEM((heads_here, 8, block), jnp.float32),
            pltpu.VMEM((heads_here, block, HEAD_DIM), jnp.float32),
            pltpu.VMEM((heads_here, block, HEAD_DIM), jnp.float32),
            pltpu.SemaphoreType.DMA((4, heads_here)),
            pltpu.SemaphoreType.DMA((3, heads_here)),
            pltpu.SemaphoreType.DMA((3, heads_here, group)),
            pltpu.SemaphoreType.DMA((4, heads_here)),
            pltpu.SemaphoreType.DMA((4, heads_here)),
            pltpu.SemaphoreType.DMA((heads_here,)),
            pltpu.SemaphoreType.DMA((heads_here,)),
            pltpu.SemaphoreType.REGULAR,
            pltpu.SemaphoreType.REGULAR,
            pltpu.SemaphoreType.DMA((heads_here, group)),
            pltpu.VMEM((2 * block, block), jnp.float32),
        ],
        compiler_params=pltpu.CompilerParams(collective_id=0, has_side_effects=True),
    )(queries, key_states, value_states, upstream, clip_lengths)
    return pl.pallas_call(
        store,
        out_shape=(out,) * 4,
        in_specs=[vmem] * 4,
        out_specs=(hbm,) * 4,
        scratch_shapes=[pltpu.SemaphoreType.DMA((4, 2))],
    )(*[pltpu.with_memory_space_constraint(r, pltpu.VMEM) for r in results])


def solution(mesh):
    return jax.shard_map(
        on_device,
        mesh=mesh,
        in_specs=(
            P(("dp", "blk", "head"), None),
            P(("dp", "blk", "head"), None),
            P(("dp", "blk", "head"), None),
            P(("dp", "blk"), "head"),
            P("dp"),
        ),
        out_specs=(P(("dp", "blk"), "head"),) * 4,
        check_vma=False,
    )
```
